32 devices in a mesh: groups: 1, row: 8 (over z, y), col: 2 (over x), chan: 2 (over core).
Axes of the slice: x: 2, y: 2, z: 4, core: 2. Of those that a mesh axis runs over, the one named last changes fastest.
Arguments:
- pair: bfloat16 [256, 128, 256], P(('groups', 'row'), None, 'col'), may hold values from -6 to 6
- grad_x: bfloat16 [256, 128, 256], P(('groups', 'row'), 'chan', 'col'), may hold values from -0.375 to 0.375
- ln_gain: float32 [128], replicated, may hold values from 0.5 to 1.5
- ln_bias: float32 [128], replicated, may hold values from -3 to 3
- weights: bfloat16 [4, 128, 128], P(None, None, 'chan'), may hold values from -0.5 to 0.5
- chain_id: int32 [256], P('groups'), may hold values from 0 to 15, never falling along the last dimension, each value on 1 to 32 neighbouring positions
- kept: int32 [16, 16], P('groups'), may hold values 0 or 1
Outputs:
- grad_pair: float32 [256, 128, 256], P(('groups', 'row'), 'chan', 'col')
The draws below stay inside these ranges and needn't reach their ends.
Inputs may be any that keep to these rules, and one draw needn't show every extreme that they name: `chain_id`: chain numbers never fall along the residues; each chain holds 1 to 32 residues.
All inputs are finite; a program needn't handle non-finite values.
Results may differ from the reference program's by a relative error of at most 0.0055.
Values may be sent and summed in bfloat16 or wider, within the bound.
A program may use at most 128 MiB of HBM per device.

```python
import math
import jax
import jax.numpy as jnp
import numpy as np
from jax import lax

C = 128
H = 128
NCH = 16
N = 256
CHAIN_MOST = 32


def with_ends(entries, key, least, high):
    spot = [jax.random.randint(jax.random.fold_in(key, axis), (), 0, length) for axis, length in enumerate(entries.shape)]
    longest = entries.shape.index(max(entries.shape))
    beside = spot[:longest] + [(spot[longest] + 1) % entries.shape[longest]] + spot[longest + 1:]
    return entries.at[tuple(spot)].set(least).at[tuple(beside)].set(high)


def block_levels(stream_key, shape, shards, low, high):
    def one(axis_at, parts):
        steps = jax.random.uniform(jax.random.fold_in(jax.random.fold_in(stream_key, 6), axis_at), (parts,), jnp.float32, low / len(shards), high / len(shards))
        return jnp.repeat(jnp.exp(steps), shape[axis_at] // parts).reshape((-1,) + (1,) * (len(shape) - axis_at - 1))

    loudness = one(*shards[0])
    for cut in shards[1:]:
        loudness = loudness * one(*cut)
    return loudness


def split_up(number_of, total, reach, slope):
    loads = [(1 << 20) // math.isqrt(grade ** slope) + 1 for grade in range(2, number_of + 1)]
    rest, holding = total - reach - (number_of - 1), [1] * (number_of - 1)
    while rest > 0:
        candidates = [i for i in range(number_of - 1) if holding[i] < reach]
        whole, remaining = sum([loads[i] for i in candidates]), rest
        for i in candidates:
            extra = min(reach - holding[i], max(1, remaining * loads[i] // whole), rest)
            holding[i] = holding[i] + extra
            rest = rest - extra
    return np.array([reach] + holding)


def uneven(rng, amount, total, bound, lean):
    if amount == 2:
        one = jax.random.randint(rng, (), max(1, total - bound), min(bound, total - 1) + 1)
        return jnp.stack([one, total - one])
    lengths = jnp.asarray(split_up(amount, total, bound, lean), jnp.int32)
    twos = (amount - 1) // 2
    giver, sink = lengths[1:1 + 2 * twos:2], lengths[2:2 + 2 * twos:2]
    room = jnp.minimum(giver - 1, bound - sink)
    shifted = jax.random.randint(jax.random.fold_in(rng, 1), (twos,), 0, 1 << 20) % (room + 1)
    lengths = lengths.at[1:1 + 2 * twos:2].set(giver - shifted).at[2:2 + 2 * twos:2].set(sink + shifted)
    return lengths[jax.random.permutation(jax.random.fold_in(rng, 2), amount)]


def scatter_about(own_key, extent, scale, limit, split=(), kind=jnp.bfloat16):
    array = jax.random.normal(own_key, extent, jnp.float32) * scale
    if len(split) > 0:
        array = block_levels(own_key, extent, split, -0.22, 0.18) * array
    return jnp.clip(array, min=-limit, max=limit).astype(kind)


def setup_inputs(seed: int = 0, part: int = 0) -> dict:
    streams_of = jax.random.split(jax.random.key(seed), 8)
    own_keys = jax.random.split(jax.random.fold_in(streams_of[7], part), 8)
    return {
        "pair": scatter_about(own_keys[0], (N, C, N), 1.0, 6.0, ((0, 8), (2, 2))),
        "grad_x": scatter_about(own_keys[1], (N, H, N), 0.0625, 0.375, ((0, 8), (1, 2), (2, 2))),
        "ln_gain": jnp.clip(1.0 + 0.1 * jax.random.normal(streams_of[2], (C,), jnp.float32), 0.5, 1.5),
        "ln_bias": scatter_about(streams_of[3], (C,), 0.5, 3.0, (), jnp.float32),
        "weights": scatter_about(streams_of[4], (4, C, H), C ** -0.5, 0.5, ((2, 2),)),
        "chain_id": jnp.searchsorted(jnp.cumsum(uneven(own_keys[5], NCH, N, CHAIN_MOST, 2)), jnp.arange(N), side="right").astype(jnp.int32),
        "kept": with_ends((jax.random.randint(own_keys[6], (NCH, NCH), 0, 2) < 1).astype(jnp.int32), jax.random.fold_in(own_keys[6], 1), 0, 1),
    }


def normalize(pair, ln_gain, ln_bias):
    values = pair.astype(jnp.float32)
    centered = values - lax.optimization_barrier(jnp.mean(values, axis=1, keepdims=True))
    inverse = lax.rsqrt(lax.optimization_barrier(jnp.mean(centered * centered, axis=1, keepdims=True)) + 1e-05)
    standard = centered * inverse
    normed = (standard * ln_gain[None, :, None] + ln_bias[None, :, None]).astype(jnp.bfloat16)
    return (standard, inverse, normed)

def norm_backward(grad_norm, standard, inverse, ln_gain):
    scaled = grad_norm * ln_gain[None, :, None]
    centered = scaled - lax.optimization_barrier(jnp.mean(scaled, axis=1, keepdims=True))
    return (centered - standard * lax.optimization_barrier(jnp.mean(scaled * standard, axis=1, keepdims=True))) * inverse

def reference(pair, grad_x, ln_gain, ln_bias, weights, chain_id, kept):
    standard, inverse, normed = normalize(pair, ln_gain, ln_bias)
    chain_hot = (chain_id[:, None] == jnp.arange(kept.shape[0], dtype=jnp.int32)[None, :]).astype(jnp.float32)
    reached = jnp.dot(chain_hot, kept.astype(jnp.float32), preferred_element_type=jnp.float32)
    pair_mask = jnp.dot(reached, chain_hot.T, preferred_element_type=jnp.float32)
    mask_three = pair_mask[:, None, :]
    normed_wide = normed.astype(jnp.float32)
    weights_wide = weights.astype(jnp.float32)
    left_value = jnp.einsum('ick,ch->ihk', normed_wide, weights_wide[0])
    left_gate = jax.nn.sigmoid(jnp.einsum('ick,ch->ihk', normed_wide, weights_wide[1]))
    right_value = jnp.einsum('ick,ch->ihk', normed_wide, weights_wide[2])
    right_gate = jax.nn.sigmoid(jnp.einsum('ick,ch->ihk', normed_wide, weights_wide[3]))
    left_side = (mask_three * left_gate * left_value).astype(jnp.bfloat16)
    right_side = (mask_three * right_gate * right_value).astype(jnp.bfloat16)
    grad_wide = grad_x.astype(jnp.float32)
    grad_left = jnp.einsum('ihj,jhk->ihk', grad_wide, right_side.astype(jnp.float32))
    grad_right = jnp.einsum('ihj,ihk->jhk', grad_wide, left_side.astype(jnp.float32))
    stack_one = (grad_left * mask_three * left_gate).astype(jnp.bfloat16).astype(jnp.float32)
    stack_two = (grad_left * mask_three * left_value * left_gate * (1.0 - left_gate)).astype(jnp.bfloat16).astype(jnp.float32)
    stack_three = (grad_right * mask_three * right_gate).astype(jnp.bfloat16).astype(jnp.float32)
    stack_four = (grad_right * mask_three * right_value * right_gate * (1.0 - right_gate)).astype(jnp.bfloat16).astype(jnp.float32)
    grad_norm = jnp.einsum('ihk,ch->ick', stack_one, weights_wide[0])
    grad_norm = grad_norm + jnp.einsum('ihk,ch->ick', stack_two, weights_wide[1])
    grad_norm = grad_norm + jnp.einsum('ihk,ch->ick', stack_three, weights_wide[2])
    grad_norm = grad_norm + jnp.einsum('ihk,ch->ick', stack_four, weights_wide[3])
    return norm_backward(grad_norm, standard, inverse, ln_gain)
```

```python
import functools
import math

import jax
import jax.numpy as jnp
from jax import lax
from jax.experimental import pallas as pl
from jax.experimental.pallas import tpu as pltpu
from jax.sharding import PartitionSpec as P

MESH = pl.DeviceIdType.MESH
F32 = jnp.float32
BF16 = jnp.bfloat16
CHUNKS = 4
SPARE = 4 << 20


def normalized(pair_ref, i):
    values = pair_ref[i].astype(F32)
    mean = jnp.mean(values, axis=0, keepdims=True)
    centered = values - mean
    inverse = lax.rsqrt(jnp.mean(centered * centered, axis=0, keepdims=True) + 1e-05)
    return mean, centered, inverse


def main_kernel(
    dims,
    pair_hbm,
    grad_hbm,
    gain_hbm,
    bias_hbm,
    proj_hbm,
    chain_hbm,
    kept_hbm,
    out_ref,
    pair_ref,
    grad_ref,
    gain_ref,
    bias_ref,
    proj_ref,
    chain_ref,
    kept_ref,
    full,
    left,
    right,
    grad_in,
    grad_wide,
    packed,
    packed_all,
    mask_ref,
    grad_left,
    grad_right,
    stat_buf,
    scaled_in,
    stat_in,
    load_sem,
    token,
    ring_send,
    ring_recv,
    cross_send,
    pass_send,
    pass_recv,
    x_send,
    x_recv,
    a_send,
    a_recv,
    swap_send,
    swap_recv,
    end_send,
    end_recv,
):
    R, X, A = dims
    rows, width, cols = pair_ref.shape
    hidden = grad_ref.shape[1]
    pack = cols // rows
    groups = packed.shape[1]
    total = R * rows
    pitch = left.shape[0] // hidden
    gpitch = grad_wide.shape[1] // rows
    half = rows // A
    step_rows = half // CHUNKS
    T = R // 2
    last = T - 1
    share = width // A

    g = lax.axis_index("groups")
    r = lax.axis_index("row")
    x = lax.axis_index("col")
    a = lax.axis_index("chan")
    sib = 1 - a

    def row_of(p):
        p = (p + R) % R
        return jnp.where(p < T, 2 * p, 2 * (R - 1 - p) + 1)

    p = jnp.where(r % 2 == 0, r // 2, R - 1 - r // 2)
    nxt = row_of(p + 1)
    prv = row_of(p - 1)

    barrier = pltpu.get_barrier_semaphore()
    peers = [(g, r, x, sib)]
    peers += [(g, r, (x + d) % X, a) for d in range(1, X)]
    peers += [(g, nxt, x, a)]
    if R > 2:
        peers += [(g, prv, x, a)]
    mirror = R - 1 - p
    to_mirror = (g, row_of(mirror), x, a)
    if T > 2:
        peers += [to_mirror]
    for peer in peers:
        pl.semaphore_signal(barrier, inc=1, device_id=peer, device_id_type=MESH)

    def load(n, src, dst):
        return pltpu.make_async_copy(src, dst, load_sem.at[n])

    own = pl.ds(a * half, half)
    other = pl.ds(sib * half, half)
    loads = [
        load(0, gain_hbm, gain_ref),
        load(1, bias_hbm, bias_ref),
        load(2, pair_hbm.at[own], pair_ref.at[own]),
        load(3, pair_hbm.at[other], pair_ref.at[other]),
        load(4, grad_hbm, grad_ref),
        load(5, proj_hbm, proj_ref),
        load(6, chain_hbm, chain_ref),
        load(7, kept_hbm, kept_ref),
    ]
    for one in loads:
        one.start()
    for one in loads[:3]:
        one.wait()

    gain = jnp.broadcast_to(gain_ref[...], (cols, width)).T
    bias = jnp.broadcast_to(bias_ref[...], (cols, width)).T

    def normalize(core, l, carry):
        i = core * half + l
        mean, centered, inverse = normalized(pair_ref, i)
        full[r, i] = ((centered * inverse) * gain + bias).astype(BF16)
        return carry

    lax.fori_loop(0, half, functools.partial(normalize, a), 0, unroll=4)
    pl.semaphore_wait(barrier, len(peers))

    def ring(t, c, forward):
        block = row_of(p - t) if forward else row_of(p + t)
        at = full.at[block, pl.ds(a * half + c * step_rows, step_rows)]
        return pltpu.make_async_remote_copy(
            src_ref=at,
            dst_ref=at,
            send_sem=ring_send.at[0 if forward else 1, t, c],
            recv_sem=ring_recv.at[0 if forward else 1, t, c],
            device_id=(g, nxt if forward else prv, x, a),
            device_id_type=MESH,
        )

    def got(t, c, forward):
        block = row_of(p - 1 - t) if forward else row_of(p + 1 + t)
        at = full.at[block, pl.ds(a * half + c * step_rows, step_rows)]
        return pltpu.make_async_copy(at, at, ring_recv.at[0 if forward else 1, t, c])

    def corner(q):
        q = (q + R) % R
        return jnp.logical_or(
            jnp.logical_or(q == 0, q == R - 1), jnp.logical_or(q == T - 1, q == T)
        )

    apart = (mirror + T - p + R) % R
    across = jnp.logical_not(corner(p))
    cross_forward = jnp.logical_and(across, apart > T)
    cross_backward = jnp.logical_and(across, apart < T)
    cross_step = jnp.where(apart > T, R - apart, apart) - 1

    def cross(c):
        at = full.at[row_of(mirror + T), pl.ds(a * half + c * step_rows, step_rows)]
        return pltpu.make_async_remote_copy(
            src_ref=at,
            dst_ref=at,
            send_sem=cross_send.at[c],
            recv_sem=ring_recv.at[c // (CHUNKS // 2), last, c],
            device_id=to_mirror,
            device_id_type=MESH,
        )

    def passed(t, c, forward, core):
        block = row_of(p - 1 - t) if forward else row_of(p + 1 + t)
        at = full.at[block, pl.ds(core * half + c * step_rows, step_rows)]
        side = 0 if forward else 1
        return pltpu.make_async_remote_copy(
            src_ref=at,
            dst_ref=at,
            send_sem=pass_send.at[side, t, c],
            recv_sem=pass_recv.at[side, t, c],
            device_id=(g, r, x, sib),
            device_id_type=MESH,
        )

    def beside(d):
        return pltpu.make_async_remote_copy(
            src_ref=grad_hbm,
            dst_ref=grad_in.at[d - 1],
            send_sem=x_send.at[d - 1],
            recv_sem=x_recv.at[d - 1],
            device_id=(g, r, (x + d) % X, a),
            device_id_type=MESH,
        )

    for c in range(CHUNKS):
        if T > 1 or c < CHUNKS // 2:
            ring(0, c, True).start()
        if T > 1 or c >= CHUNKS // 2:
            ring(0, c, False).start()
    for d in range(1, X):
        beside(d).start()

    def signal_token(k):
        pl.semaphore_signal(token.at[0, k], inc=1, device_id=(g, nxt, x, a), device_id_type=MESH)
        pl.semaphore_signal(token.at[1, k], inc=1, device_id=(g, prv, x, a), device_id_type=MESH)

    def relay(k):
        pl.semaphore_wait(token.at[0, k], 1)
        pl.semaphore_wait(token.at[1, k], 1)

        @pl.when(k + 1 < last)
        def _():
            signal_token(k + 1)

    if last > 0:
        signal_token(0)

    for one in loads[3:]:
        one.wait()
    lax.fori_loop(0, half, functools.partial(normalize, sib), 0, unroll=4)

    chains = kept_ref.shape[0]
    number = lax.broadcasted_iota(jnp.int32, (chains, total), 0)
    row_hot = (number == chain_ref[...]).astype(F32).astype(BF16)
    mine = chain_ref[:, pl.ds(pl.multiple_of(x * cols, cols), cols)]
    number = lax.broadcasted_iota(jnp.int32, (chains, cols), 0)
    col_hot = (number == mine).astype(F32).astype(BF16)
    reach = jnp.dot(kept_ref[...].astype(F32).astype(BF16), col_hot, preferred_element_type=F32)
    mask_ref[...] = lax.dot_general(
        row_hot, reach.astype(BF16), (((0,), (0,)), ((), ())), preferred_element_type=F32
    )

    projection = proj_ref[...]

    def sides(block, l):
        at = block * rows + l
        out = jnp.dot(projection, full[block, l], preferred_element_type=F32)
        mask = mask_ref[pl.ds(at, 1), :]
        lv = mask * jax.nn.sigmoid(out[hidden : 2 * hidden]) * out[:hidden]
        rv = mask * jax.nn.sigmoid(out[3 * hidden :]) * out[2 * hidden : 3 * hidden]
        left[pl.ds(at, hidden, stride=pitch), :] = lv
        right[pl.ds(at, hidden, stride=pitch), :] = rv

    def own_rows(i, carry):
        sides(r, i)
        return carry

    lax.fori_loop(0, rows, own_rows, 0, unroll=4)

    def widen_own(i, carry):
        at = pl.ds(pl.multiple_of(i * gpitch, 8), hidden)
        grad_wide[x, at, :] = grad_ref[i].astype(F32)
        return carry

    lax.fori_loop(0, rows, widen_own, 0)

    def bwd_chunk(t, c):
        return jnp.where(t < last, c, c + CHUNKS // 2)

    def unit(u):
        t = u // CHUNKS
        c = u % CHUNKS
        cb = bwd_chunk(t, c)
        passed(t, c, True, sib).wait_recv()
        passed(t, cb, False, sib).wait_recv()
        fblock = row_of(p - 1 - t)
        bblock = row_of(p + 1 + t)

        def body(l, carry):
            for core in range(A):
                sides(fblock, core * half + c * step_rows + l)
                sides(bblock, core * half + cb * step_rows + l)
            return carry

        lax.fori_loop(0, step_rows, body, 0, unroll=2)

    units = last * CHUNKS + CHUNKS // 2

    def more(t, c, forward):
        split = c < CHUNKS // 2 if forward else c >= CHUNKS // 2
        split = jnp.logical_and(split, corner(p + 1 if forward else p - 1))
        return jnp.logical_or(t + 1 < last, jnp.logical_and(t + 1 == last, split))

    def ring_step(u, carry):
        t = u // CHUNKS
        c = u % CHUNKS
        cb = bwd_chunk(t, c)
        got(t, c, True).wait()

        @pl.when(more(t, c, True))
        def _():
            ring(t + 1, c, True).start()

        @pl.when(jnp.logical_and(cross_forward, t == cross_step))
        def _():
            cross(c).start()

        passed(t, c, True, a).start()
        got(t, cb, False).wait()

        @pl.when(more(t, cb, False))
        def _():
            ring(t + 1, cb, False).start()

        @pl.when(jnp.logical_and(cross_backward, t == cross_step))
        def _():
            cross(cb).start()

        passed(t, cb, False, a).start()

        @pl.when(u < last)
        def _():
            relay(u)

        @pl.when(u > 0)
        def _():
            unit(u - 1)

        return carry

    def piece(d):
        to = (r + d) % R
        return pltpu.make_async_remote_copy(
            src_ref=packed.at[to],
            dst_ref=packed_all.at[x, r],
            send_sem=a_send.at[d],
            recv_sem=a_recv.at[d],
            device_id=(g, to, x, a),
            device_id_type=MESH,
        )

    def swap(d, s, col):
        at = packed_all.at[col, s]
        return pltpu.make_async_remote_copy(
            src_ref=at,
            dst_ref=at,
            send_sem=swap_send.at[d, s],
            recv_sem=swap_recv.at[d, s],
            device_id=(g, r, (x + d) % X, a),
            device_id_type=MESH,
        )

    first = min(max(CHUNKS, last), units)
    lax.fori_loop(0, first, ring_step, 0)

    for d in range(1, X):
        source = (x + X - d) % X
        beside(d).wait_recv()

        def widen(i, carry):
            at = pl.ds(pl.multiple_of(i * gpitch, 8), hidden)
            grad_wide[source, at, :] = grad_in[d - 1, i].astype(F32)
            return carry

        lax.fori_loop(0, rows, widen, 0)

    def pack_group(k, carry):
        for e in range(X):
            slabs = [
                grad_wide[e, pl.ds((x * groups + k) * pack + m, rows, stride=gpitch), :]
                for m in range(pack)
            ]
            for q in range(pack):
                tile = jnp.concatenate([slab[:, q * rows : (q + 1) * rows] for slab in slabs], axis=1)
                packed[e * pack + q, k] = tile.astype(BF16)
        return carry

    lax.fori_loop(0, groups, pack_group, 0)
    for d in range(1, R):
        piece(d).start()
    packed_all[x, r] = packed[r]

    third = first + (units - first) * 2 // 5
    lax.fori_loop(first, third, ring_step, 0)
    for d in range(1, X):
        swap(d, r, x).start()
    for d0 in range(1, R):
        s = (r + R - d0) % R
        at = packed_all.at[x, s]
        pltpu.make_async_copy(at, at, a_recv.at[d0]).wait()
        for d in range(1, X):
            swap(d, s, x).start()

    lax.fori_loop(third, units, ring_step, 0)
    unit(units - 1)

    for d in range(1, X):
        for s in range(R):
            swap(d, s, (x + X - d) % X).wait_recv()

    def group(k, carry):
        e = k // groups
        k2 = k % groups
        stacked = jnp.concatenate([packed_all[e, s, k2] for s in range(R)], axis=0)
        turned = stacked.T
        for m in range(pack):
            h = k * pack + m
            rh = right[pl.ds(pl.multiple_of(h * pitch, 8), total), :].astype(BF16)
            lh = left[pl.ds(pl.multiple_of(h * pitch, 8), total), :].astype(BF16)
            gx = jnp.concatenate(
                [grad_wide[e2, pl.ds(h, rows, stride=gpitch), :] for e2 in range(X)], axis=1
            ).astype(BF16)
            at = pl.ds(pl.multiple_of(h * rows, 8), rows)
            grad_left[at, :] = jnp.dot(gx, rh, preferred_element_type=F32)
            grad_right[at, :] = jnp.dot(
                turned[m * rows : (m + 1) * rows], lh, preferred_element_type=F32
            )
        return carry

    lax.fori_loop(0, groups * X, group, 0, unroll=4)

    back = projection.astype(F32).T.astype(BF16)
    n = rows // 4

    def send_end(b):
        at = pl.ds(b * n, n)
        return (
            pltpu.make_async_remote_copy(
                src_ref=left.at[pl.ds(pl.multiple_of((sib * rows + b * n) * share, 8), n * share)],
                dst_ref=scaled_in.at[pl.ds(b * n * share, n * share)],
                send_sem=end_send.at[0, b],
                recv_sem=end_recv.at[0, b],
                device_id=(g, r, x, sib),
                device_id_type=MESH,
            ),
            pltpu.make_async_remote_copy(
                src_ref=stat_buf.at[at],
                dst_ref=stat_in.at[at],
                send_sem=end_send.at[1, b],
                recv_sem=end_recv.at[1, b],
                device_id=(g, r, x, sib),
                device_id_type=MESH,
            ),
        )

    def finish_row(i, carry):
        out = jnp.dot(projection, full[r, i], preferred_element_type=F32)
        mask = mask_ref[pl.ds(r * rows + i, 1), :]
        gl = grad_left[pl.ds(i, hidden, stride=rows), :] * mask
        gr = grad_right[pl.ds(i, hidden, stride=rows), :] * mask
        s0 = jax.nn.sigmoid(out[hidden : 2 * hidden])
        s1 = jax.nn.sigmoid(out[3 * hidden :])
        gl = gl * s0
        gr = gr * s1
        stack = jnp.concatenate(
            [
                gl.astype(BF16),
                (gl * out[:hidden] * (1.0 - s0)).astype(BF16),
                gr.astype(BF16),
                (gr * out[2 * hidden : 3 * hidden] * (1.0 - s1)).astype(BF16),
            ],
            axis=0,
        )
        scaled = jnp.dot(back, stack, preferred_element_type=F32) * gain
        mean, centered, inverse = normalized(pair_ref, i)
        for part in range(A):
            at = pl.ds(pl.multiple_of((part * rows + i) * share, 8), share)
            left[at, :] = scaled[part * share : (part + 1) * share]
        one = jnp.sum(scaled, axis=0, keepdims=True)
        two = jnp.sum(scaled * centered, axis=0, keepdims=True) * inverse
        stat_buf[i] = jnp.concatenate([one, two, mean, inverse, one, one, one, one], axis=0)
        return carry

    for b in range(4):
        lax.fori_loop(b * n, (b + 1) * n, finish_row, 0, unroll=8)
        for copy in send_end(b):
            copy.start()

    for b in range(4):
        for copy in send_end(b):
            copy.wait()

        def combine(i, carry):
            kept_at = pl.ds(pl.multiple_of((a * rows + i) * share, 8), share)
            in_at = pl.ds(pl.multiple_of(i * share, 8), share)
            whole = left[kept_at, :] + scaled_in[in_at, :]
            stats = stat_buf[i]
            other = stat_in[i]
            one = (stats[0:1] + other[0:1]) * (1.0 / width)
            two = (stats[1:2] + other[1:2]) * (1.0 / width)
            inverse = stats[3:4]
            values = pair_ref[i, pl.ds(pl.multiple_of(a * share, 16), share), :].astype(F32)
            standard = (values - stats[2:3]) * inverse
            out_ref[i] = (whole - one - standard * two) * inverse
            return carry

        lax.fori_loop(b * n, (b + 1) * n, combine, 0, unroll=8)

    for d in range(1, R):
        piece(d).wait_send()
    for d in range(1, X):
        beside(d).wait_send()
        for s in range(R):
            swap(d, s, x).wait_send()
    for c in range(CHUNKS):
        if T > 1 or c < CHUNKS // 2:
            ring(0, c, True).wait_send()
        if T > 1 or c >= CHUNKS // 2:
            ring(0, c, False).wait_send()

    @pl.when(across)
    def _():
        for c in range(CHUNKS):
            cross(c).wait_send()

    def drain(u, carry):
        t = u // CHUNKS
        c = u % CHUNKS
        cb = bwd_chunk(t, c)

        @pl.when(more(t, c, True))
        def _():
            ring(t + 1, c, True).wait_send()

        @pl.when(more(t, cb, False))
        def _():
            ring(t + 1, cb, False).wait_send()

        passed(t, c, True, a).wait_send()
        passed(t, cb, False, a).wait_send()
        return carry

    lax.fori_loop(0, units, drain, 0)


def local(dims, pair, grad_x, ln_gain, ln_bias, weights, chain_id, kept):
    R, X, A = dims
    rows, width, cols = pair.shape
    hidden = grad_x.shape[1]
    total = R * rows
    pack = cols // rows
    groups = hidden // (pack * X)
    pitch = total + 8
    gpitch = hidden + 8
    vmem = pl.BlockSpec(memory_space=pltpu.VMEM)
    hbm = pl.BlockSpec(memory_space=pltpu.HBM)
    proj = jnp.transpose(weights, (0, 2, 1)).reshape(4 * hidden, width)
    T = R // 2
    dma = pltpu.SemaphoreType.DMA
    args = (pair, grad_x, ln_gain[None, :], ln_bias[None, :], proj, chain_id[None, :], kept)
    buffers = [pltpu.VMEM(arg.shape, arg.dtype) for arg in args] + [
        pltpu.VMEM((R, rows, width, cols), BF16),
        pltpu.VMEM((hidden * pitch, cols), F32),
        pltpu.VMEM((hidden * pitch, cols), F32),
        pltpu.VMEM((max(X - 1, 1), rows, hidden, cols), BF16),
        pltpu.VMEM((X, rows * gpitch, cols), F32),
        pltpu.VMEM((R, groups, rows, cols), BF16),
        pltpu.VMEM((X, R, groups, rows, cols), BF16),
        pltpu.VMEM((total, cols), F32),
        pltpu.VMEM((hidden * rows, cols), F32),
        pltpu.VMEM((hidden * rows, cols), F32),
        pltpu.VMEM((rows, 8, cols), F32),
        pltpu.VMEM((rows * (width // A), cols), F32),
        pltpu.VMEM((rows, 8, cols), F32),
    ]
    need = sum(math.prod(one.shape) * jnp.dtype(one.dtype).itemsize for one in buffers)
    return pl.pallas_call(
        functools.partial(main_kernel, dims),
        out_shape=jax.ShapeDtypeStruct((rows, width // A, cols), F32),
        in_specs=[hbm] * 7,
        out_specs=vmem,
        scratch_shapes=buffers + [
            dma((8,)),
            pltpu.SemaphoreType.REGULAR((2, T)),
            dma((2, T, CHUNKS)),
            dma((2, T, CHUNKS)),
            dma((CHUNKS,)),
            dma((2, T, CHUNKS)),
            dma((2, T, CHUNKS)),
            dma((X,)),
            dma((X,)),
            dma((R,)),
            dma((R,)),
            dma((X, R)),
            dma((X, R)),
            dma((2, 4)),
            dma((2, 4)),
        ],
        compiler_params=pltpu.CompilerParams(
            collective_id=0, has_side_effects=True, vmem_limit_bytes=min(67043328, need + SPARE)
        ),
    )(*args)


def solution(mesh):
    placed = (
        P(("groups", "row"), None, "col"),
        P(("groups", "row"), "chan", "col"),
        P(),
        P(),
        P(None, None, "chan"),
        P("groups"),
        P("groups", None),
    )
    dims = (mesh.shape["row"], mesh.shape["col"], mesh.shape["chan"])
    return jax.shard_map(
        functools.partial(local, dims),
        mesh=mesh,
        in_specs=placed,
        out_specs=P(("groups", "row"), "chan", "col"),
        check_vma=False,
    )
```

```python
import functools
import math

import jax
import jax.numpy as jnp
from jax import lax
from jax.experimental import pallas as pl
from jax.experimental.pallas import tpu as pltpu
from jax.sharding import PartitionSpec as P

MESH = pl.DeviceIdType.MESH
F32 = jnp.float32
BF16 = jnp.bfloat16
CHUNKS = 4
SPARE = 4 << 20


def normalized(pair_ref, i):
    values = pair_ref[i].astype(F32)
    mean = jnp.mean(values, axis=0, keepdims=True)
    centered = values - mean
    inverse = lax.rsqrt(jnp.mean(centered * centered, axis=0, keepdims=True) + 1e-05)
    return mean, centered, inverse


def main_kernel(
    dims,
    pair_hbm,
    grad_hbm,
    gain_hbm,
    bias_hbm,
    proj_hbm,
    chain_hbm,
    kept_hbm,
    out_ref,
    pair_ref,
    grad_ref,
    gain_ref,
    bias_ref,
    proj_ref,
    chain_ref,
    kept_ref,
    full,
    left,
    right,
    grad_in,
    grad_wide,
    packed,
    packed_all,
    mask_ref,
    grad_left,
    grad_right,
    stat_buf,
    scaled_in,
    stat_in,
    load_sem,
    token,
    ring_send,
    ring_recv,
    cross_send,
    pass_send,
    pass_recv,
    x_send,
    x_recv,
    a_send,
    a_recv,
    swap_send,
    swap_recv,
    end_send,
    end_recv,
):
    R, X, A = dims
    rows, width, cols = pair_ref.shape
    hidden = grad_ref.shape[1]
    pack = cols // rows
    groups = packed.shape[1]
    total = R * rows
    pitch = left.shape[0] // hidden
    gpitch = grad_wide.shape[1] // rows
    half = rows // A
    step_rows = half // CHUNKS
    T = R // 2
    last = T - 1
    share = width // A

    g = lax.axis_index("groups")
    r = lax.axis_index("row")
    x = lax.axis_index("col")
    a = lax.axis_index("chan")
    sib = 1 - a

    def row_of(p):
        p = (p + R) % R
        return jnp.where(p < T, 2 * p, 2 * (R - 1 - p) + 1)

    p = jnp.where(r % 2 == 0, r // 2, R - 1 - r // 2)
    nxt = row_of(p + 1)
    prv = row_of(p - 1)

    barrier = pltpu.get_barrier_semaphore()
    peers = [(g, r, x, sib)]
    peers += [(g, r, (x + d) % X, a) for d in range(1, X)]
    peers += [(g, nxt, x, a)]
    if R > 2:
        peers += [(g, prv, x, a)]
    mirror = R - 1 - p
    to_mirror = (g, row_of(mirror), x, a)
    if T > 2:
        peers += [to_mirror]
    for peer in peers:
        pl.semaphore_signal(barrier, inc=1, device_id=peer, device_id_type=MESH)

    def load(n, src, dst):
        return pltpu.make_async_copy(src, dst, load_sem.at[n])

    own = pl.ds(a * half, half)
    other = pl.ds(sib * half, half)
    loads = [
        load(0, gain_hbm, gain_ref),
        load(1, bias_hbm, bias_ref),
        load(2, pair_hbm.at[own], pair_ref.at[own]),
        load(3, pair_hbm.at[other], pair_ref.at[other]),
        load(4, grad_hbm, grad_ref),
        load(5, proj_hbm, proj_ref),
        load(6, chain_hbm, chain_ref),
        load(7, kept_hbm, kept_ref),
    ]
    for one in loads:
        one.start()
    for one in loads[:3]:
        one.wait()

    gain = jnp.broadcast_to(gain_ref[...], (cols, width)).T
    bias = jnp.broadcast_to(bias_ref[...], (cols, width)).T

    def normalize(core, l, carry):
        i = core * half + l
        mean, centered, inverse = normalized(pair_ref, i)
        full[r, i] = ((centered * inverse) * gain + bias).astype(BF16)
        return carry

    lax.fori_loop(0, half, functools.partial(normalize, a), 0, unroll=4)
    pl.semaphore_wait(barrier, len(peers))

    def ring(t, c, forward):
        block = row_of(p - t) if forward else row_of(p + t)
        at = full.at[block, pl.ds(a * half + c * step_rows, step_rows)]
        return pltpu.make_async_remote_copy(
            src_ref=at,
            dst_ref=at,
            send_sem=ring_send.at[0 if forward else 1, t, c],
            recv_sem=ring_recv.at[0 if forward else 1, t, c],
            device_id=(g, nxt if forward else prv, x, a),
            device_id_type=MESH,
        )

    def got(t, c, forward):
        block = row_of(p - 1 - t) if forward else row_of(p + 1 + t)
        at = full.at[block, pl.ds(a * half + c * step_rows, step_rows)]
        return pltpu.make_async_copy(at, at, ring_recv.at[0 if forward else 1, t, c])

    def corner(q):
        q = (q + R) % R
        return jnp.logical_or(
            jnp.logical_or(q == 0, q == R - 1), jnp.logical_or(q == T - 1, q == T)
        )

    apart = (mirror + T - p + R) % R
    across = jnp.logical_not(corner(p))
    cross_forward = jnp.logical_and(across, apart > T)
    cross_backward = jnp.logical_and(across, apart < T)
    cross_step = jnp.where(apart > T, R - apart, apart) - 1

    def cross(c):
        at = full.at[row_of(mirror + T), pl.ds(a * half + c * step_rows, step_rows)]
        return pltpu.make_async_remote_copy(
            src_ref=at,
            dst_ref=at,
            send_sem=cross_send.at[c],
            recv_sem=ring_recv.at[c // (CHUNKS // 2), last, c],
            device_id=to_mirror,
            device_id_type=MESH,
        )

    def passed(t, c, forward, core):
        block = row_of(p - 1 - t) if forward else row_of(p + 1 + t)
        at = full.at[block, pl.ds(core * half + c * step_rows, step_rows)]
        side = 0 if forward else 1
        return pltpu.make_async_remote_copy(
            src_ref=at,
            dst_ref=at,
            send_sem=pass_send.at[side, t, c],
            recv_sem=pass_recv.at[side, t, c],
            device_id=(g, r, x, sib),
            device_id_type=MESH,
        )

    def beside(d):
        return pltpu.make_async_remote_copy(
            src_ref=grad_hbm,
            dst_ref=grad_in.at[d - 1],
            send_sem=x_send.at[d - 1],
            recv_sem=x_recv.at[d - 1],
            device_id=(g, r, (x + d) % X, a),
            device_id_type=MESH,
        )

    for c in range(CHUNKS):
        if T > 1 or c < CHUNKS // 2:
            ring(0, c, True).start()
        if T > 1 or c >= CHUNKS // 2:
            ring(0, c, False).start()
    for d in range(1, X):
        beside(d).start()

    def signal_token(k):
        pl.semaphore_signal(token.at[0, k], inc=1, device_id=(g, nxt, x, a), device_id_type=MESH)
        pl.semaphore_signal(token.at[1, k], inc=1, device_id=(g, prv, x, a), device_id_type=MESH)

    def relay(k):
        pl.semaphore_wait(token.at[0, k], 1)
        pl.semaphore_wait(token.at[1, k], 1)

        @pl.when(k + 1 < last)
        def _():
            signal_token(k + 1)

    if last > 0:
        signal_token(0)

    for one in loads[3:]:
        one.wait()
    lax.fori_loop(0, half, functools.partial(normalize, sib), 0, unroll=4)

    chains = kept_ref.shape[0]
    number = lax.broadcasted_iota(jnp.int32, (chains, total), 0)
    row_hot = (number == chain_ref[...]).astype(F32).astype(BF16)
    mine = chain_ref[:, pl.ds(pl.multiple_of(x * cols, cols), cols)]
    number = lax.broadcasted_iota(jnp.int32, (chains, cols), 0)
    col_hot = (number == mine).astype(F32).astype(BF16)
    reach = jnp.dot(kept_ref[...].astype(F32).astype(BF16), col_hot, preferred_element_type=F32)
    mask_ref[...] = lax.dot_general(
        row_hot, reach.astype(BF16), (((0,), (0,)), ((), ())), preferred_element_type=F32
    )

    projection = proj_ref[...]

    def sides(block, l):
        at = block * rows + l
        out = jnp.dot(projection, full[block, l], preferred_element_type=F32)
        mask = mask_ref[pl.ds(at, 1), :]
        lv = mask * jax.nn.sigmoid(out[hidden : 2 * hidden]) * out[:hidden]
        rv = mask * jax.nn.sigmoid(out[3 * hidden :]) * out[2 * hidden : 3 * hidden]
        left[pl.ds(at, hidden, stride=pitch), :] = lv
        right[pl.ds(at, hidden, stride=pitch), :] = rv

    def own_rows(i, carry):
        sides(r, i)
        return carry

    lax.fori_loop(0, rows, own_rows, 0, unroll=4)

    def widen_own(i, carry):
        at = pl.ds(pl.multiple_of(i * gpitch, 8), hidden)
        grad_wide[x, at, :] = grad_ref[i].astype(F32)
        return carry

    lax.fori_loop(0, rows, widen_own, 0)

    def bwd_chunk(t, c):
        return jnp.where(t < last, c, c + CHUNKS // 2)

    def unit(u):
        t = u // CHUNKS
        c = u % CHUNKS
        cb = bwd_chunk(t, c)
        passed(t, c, True, sib).wait_recv()
        passed(t, cb, False, sib).wait_recv()
        fblock = row_of(p - 1 - t)
        bblock = row_of(p + 1 + t)

        def body(l, carry):
            for core in range(A):
                sides(fblock, core * half + c * step_rows + l)
                sides(bblock, core * half + cb * step_rows + l)
            return carry

        lax.fori_loop(0, step_rows, body, 0, unroll=2)

    units = last * CHUNKS + CHUNKS // 2

    def more(t, c, forward):
        split = c < CHUNKS // 2 if forward else c >= CHUNKS // 2
        split = jnp.logical_and(split, corner(p + 1 if forward else p - 1))
        return jnp.logical_or(t + 1 < last, jnp.logical_and(t + 1 == last, split))

    def ring_step(u, carry):
        t = u // CHUNKS
        c = u % CHUNKS
        cb = bwd_chunk(t, c)
        got(t, c, True).wait()

        @pl.when(more(t, c, True))
        def _():
            ring(t + 1, c, True).start()

        @pl.when(jnp.logical_and(cross_forward, t == cross_step))
        def _():
            cross(c).start()

        passed(t, c, True, a).start()
        got(t, cb, False).wait()

        @pl.when(more(t, cb, False))
        def _():
            ring(t + 1, cb, False).start()

        @pl.when(jnp.logical_and(cross_backward, t == cross_step))
        def _():
            cross(cb).start()

        passed(t, cb, False, a).start()

        @pl.when(u < last)
        def _():
            relay(u)

        @pl.when(u > 0)
        def _():
            unit(u - 1)

        return carry

    def piece(d):
        to = (r + d) % R
        return pltpu.make_async_remote_copy(
            src_ref=packed.at[to],
            dst_ref=packed_all.at[x, r],
            send_sem=a_send.at[d],
            recv_sem=a_recv.at[d],
            device_id=(g, to, x, a),
            device_id_type=MESH,
        )

    def swap(d, s, col):
        at = packed_all.at[col, s]
        return pltpu.make_async_remote_copy(
            src_ref=at,
            dst_ref=at,
            send_sem=swap_send.at[d, s],
            recv_sem=swap_recv.at[d, s],
            device_id=(g, r, (x + d) % X, a),
            device_id_type=MESH,
        )

    first = min(max(CHUNKS, last), units)
    lax.fori_loop(0, first, ring_step, 0)

    for d in range(1, X):
        source = (x + X - d) % X
        beside(d).wait_recv()

        def widen(i, carry):
            at = pl.ds(pl.multiple_of(i * gpitch, 8), hidden)
            grad_wide[source, at, :] = grad_in[d - 1, i].astype(F32)
            return carry

        lax.fori_loop(0, rows, widen, 0)

    def pack_group(k, carry):
        for e in range(X):
            slabs = [
                grad_wide[e, pl.ds((x * groups + k) * pack + m, rows, stride=gpitch), :]
                for m in range(pack)
            ]
            for q in range(pack):
                tile = jnp.concatenate([slab[:, q * rows : (q + 1) * rows] for slab in slabs], axis=1)
                packed[e * pack + q, k] = tile.astype(BF16)
        return carry

    lax.fori_loop(0, groups, pack_group, 0)
    for d in range(1, R):
        piece(d).start()
    packed_all[x, r] = packed[r]

    third = first + (units - first) * 2 // 5
    lax.fori_loop(first, third, ring_step, 0)
    for d in range(1, X):
        swap(d, r, x).start()
    for d0 in range(1, R):
        s = (r + R - d0) % R
        at = packed_all.at[x, s]
        pltpu.make_async_copy(at, at, a_recv.at[d0]).wait()
        for d in range(1, X):
            swap(d, s, x).start()

    lax.fori_loop(third, units, ring_step, 0)
    unit(units - 1)

    for d in range(1, X):
        for s in range(R):
            swap(d, s, (x + X - d) % X).wait_recv()

    def group(k, carry):
        e = k // groups
        k2 = k % groups
        stacked = jnp.concatenate([packed_all[e, s, k2] for s in range(R)], axis=0)
        turned = stacked.T
        for m in range(pack):
            h = k * pack + m
            rh = right[pl.ds(pl.multiple_of(h * pitch, 8), total), :].astype(BF16)
            lh = left[pl.ds(pl.multiple_of(h * pitch, 8), total), :].astype(BF16)
            gx = jnp.concatenate(
                [grad_wide[e2, pl.ds(h, rows, stride=gpitch), :] for e2 in range(X)], axis=1
            ).astype(BF16)
            at = pl.ds(pl.multiple_of(h * rows, 8), rows)
            grad_left[at, :] = jnp.dot(gx, rh, preferred_element_type=F32)
            grad_right[at, :] = jnp.dot(
                turned[m * rows : (m + 1) * rows], lh, preferred_element_type=F32
            )
        return carry

    lax.fori_loop(0, groups * X, group, 0, unroll=4)

    back = projection.astype(F32).T.astype(BF16)
    n = rows // 4

    def send_end(b):
        at = pl.ds(b * n, n)
        return (
            pltpu.make_async_remote_copy(
                src_ref=left.at[pl.ds(pl.multiple_of((sib * rows + b * n) * share, 8), n * share)],
                dst_ref=scaled_in.at[pl.ds(b * n * share, n * share)],
                send_sem=end_send.at[0, b],
                recv_sem=end_recv.at[0, b],
                device_id=(g, r, x, sib),
                device_id_type=MESH,
            ),
            pltpu.make_async_remote_copy(
                src_ref=stat_buf.at[at],
                dst_ref=stat_in.at[at],
                send_sem=end_send.at[1, b],
                recv_sem=end_recv.at[1, b],
                device_id=(g, r, x, sib),
                device_id_type=MESH,
            ),
        )

    def finish_row(i, carry):
        out = jnp.dot(projection, full[r, i], preferred_element_type=F32)
        mask = mask_ref[pl.ds(r * rows + i, 1), :]
        gl = grad_left[pl.ds(i, hidden, stride=rows), :] * mask
        gr = grad_right[pl.ds(i, hidden, stride=rows), :] * mask
        s0 = jax.nn.sigmoid(out[hidden : 2 * hidden])
        s1 = jax.nn.sigmoid(out[3 * hidden :])
        gl = gl * s0
        gr = gr * s1
        stack = jnp.concatenate(
            [
                gl.astype(BF16),
                (gl * out[:hidden] * (1.0 - s0)).astype(BF16),
                gr.astype(BF16),
                (gr * out[2 * hidden : 3 * hidden] * (1.0 - s1)).astype(BF16),
            ],
            axis=0,
        )
        scaled = jnp.dot(back, stack, preferred_element_type=F32) * gain
        mean, centered, inverse = normalized(pair_ref, i)
        for part in range(A):
            at = pl.ds(pl.multiple_of((part * rows + i) * share, 8), share)
            left[at, :] = scaled[part * share : (part + 1) * share]
        one = jnp.sum(scaled, axis=0, keepdims=True)
        two = jnp.sum(scaled * centered, axis=0, keepdims=True) * inverse
        stat_buf[i] = jnp.concatenate([one, two, mean, inverse, one, one, one, one], axis=0)
        return carry

    for b in range(4):
        lax.fori_loop(b * n, (b + 1) * n, finish_row, 0, unroll=8)
        for copy in send_end(b):
            copy.start()

    for b in range(4):
        for copy in send_end(b):
            copy.wait()

        def combine(i, carry):
            kept_at = pl.ds(pl.multiple_of((a * rows + i) * share, 8), share)
            in_at = pl.ds(pl.multiple_of(i * share, 8), share)
            whole = left[kept_at, :] + scaled_in[in_at, :]
            stats = stat_buf[i]
            other = stat_in[i]
            one = (stats[0:1] + other[0:1]) * (1.0 / width)
            two = (stats[1:2] + other[1:2]) * (1.0 / width)
            inverse = stats[3:4]
            values = pair_ref[i, pl.ds(pl.multiple_of(a * share, 16), share), :].astype(F32)
            standard = (values - stats[2:3]) * inverse
            out_ref[i] = (whole - one - standard * two) * inverse
            return carry

        lax.fori_loop(b * n, (b + 1) * n, combine, 0, unroll=8)

    for d in range(1, R):
        piece(d).wait_send()
    for d in range(1, X):
        beside(d).wait_send()
        for s in range(R):
            swap(d, s, x).wait_send()
    for c in range(CHUNKS):
        if T > 1 or c < CHUNKS // 2:
            ring(0, c, True).wait_send()
        if T > 1 or c >= CHUNKS // 2:
            ring(0, c, False).wait_send()

    @pl.when(across)
    def _():
        for c in range(CHUNKS):
            cross(c).wait_send()

    def drain(u, carry):
        t = u // CHUNKS
        c = u % CHUNKS
        cb = bwd_chunk(t, c)

        @pl.when(more(t, c, True))
        def _():
            ring(t + 1, c, True).wait_send()

        @pl.when(more(t, cb, False))
        def _():
            ring(t + 1, cb, False).wait_send()

        passed(t, c, True, a).wait_send()
        passed(t, cb, False, a).wait_send()
        return carry

    lax.fori_loop(0, units, drain, 0)


def local(dims, pair, grad_x, ln_gain, ln_bias, weights, chain_id, kept):
    R, X, A = dims
    rows, width, cols = pair.shape
    hidden = grad_x.shape[1]
    total = R * rows
    pack = cols // rows
    groups = hidden // (pack * X)
    pitch = total + 8
    gpitch = hidden + 8
    vmem = pl.BlockSpec(memory_space=pltpu.VMEM)
    hbm = pl.BlockSpec(memory_space=pltpu.HBM)
    proj = jnp.transpose(weights, (0, 2, 1)).reshape(4 * hidden, width)
    T = R // 2
    dma = pltpu.SemaphoreType.DMA
    args = (pair, grad_x, ln_gain[None, :], ln_bias[None, :], proj, chain_id[None, :], kept)
    buffers = [pltpu.VMEM(arg.shape, arg.dtype) for arg in args] + [
        pltpu.VMEM((R, rows, width, cols), BF16),
        pltpu.VMEM((hidden * pitch, cols), F32),
        pltpu.VMEM((hidden * pitch, cols), F32),
        pltpu.VMEM((max(X - 1, 1), rows, hidden, cols), BF16),
        pltpu.VMEM((X, rows * gpitch, cols), F32),
        pltpu.VMEM((R, groups, rows, cols), BF16),
        pltpu.VMEM((X, R, groups, rows, cols), BF16),
        pltpu.VMEM((total, cols), F32),
        pltpu.VMEM((hidden * rows, cols), F32),
        pltpu.VMEM((hidden * rows, cols), F32),
        pltpu.VMEM((rows, 8, cols), F32),
        pltpu.VMEM((rows * (width // A), cols), F32),
        pltpu.VMEM((rows, 8, cols), F32),
    ]
    need = sum(math.prod(one.shape) * jnp.dtype(one.dtype).itemsize for one in buffers)
    return pl.pallas_call(
        functools.partial(main_kernel, dims),
        out_shape=jax.ShapeDtypeStruct((rows, width // A, cols), F32),
        in_specs=[hbm] * 7,
        out_specs=vmem,
        scratch_shapes=buffers + [
            dma((8,)),
            pltpu.SemaphoreType.REGULAR((2, T)),
            dma((2, T, CHUNKS)),
            dma((2, T, CHUNKS)),
            dma((CHUNKS,)),
            dma((2, T, CHUNKS)),
            dma((2, T, CHUNKS)),
            dma((X,)),
            dma((X,)),
            dma((R,)),
            dma((R,)),
            dma((X, R)),
            dma((X, R)),
            dma((2, 4)),
            dma((2, 4)),
        ],
        compiler_params=pltpu.CompilerParams(
            collective_id=0, has_side_effects=True, vmem_limit_bytes=min(67043328, need + SPARE)
        ),
    )(*[pltpu.with_memory_space_constraint(arg, pltpu.HBM) for arg in args])


def solution(mesh):
    placed = (
        P(("groups", "row"), None, "col"),
        P(("groups", "row"), "chan", "col"),
        P(),
        P(),
        P(None, None, "chan"),
        P("groups"),
        P("groups", None),
    )
    dims = (mesh.shape["row"], mesh.shape["col"], mesh.shape["chan"])
    return jax.shard_map(
        functools.partial(local, dims),
        mesh=mesh,
        in_specs=placed,
        out_specs=P(("groups", "row"), "chan", "col"),
        check_vma=False,
    )
```
